32 devices in a mesh: dp: 2 (over y), fsdp: 16 (over z, x, core).
Axes of the slice: x: 2, y: 2, z: 4, core: 2. Of those that a mesh axis runs over, the one named last changes fastest.
Arguments:
- patches: bfloat16 [160, 197, 768], P(('dp', 'fsdp')), may hold values from -6 to 6
- patch_mask: int32 [160, 197], P(('dp', 'fsdp')), may hold values from 0 to 1, as said below
- cotangent: bfloat16 [160, 197, 768], P(('dp', 'fsdp')), may hold values from -6 to 6
- mask_token: bfloat16 [768], P(('dp', 'fsdp')), may hold values from -5 to 5
- pre_gain: bfloat16 [768], P(('dp', 'fsdp')), may hold values from 0.099609375 to 1.8984375
- pre_shift: bfloat16 [768], P(('dp', 'fsdp')), may hold values from -3 to 3
- qkv_weight: bfloat16 [1769472], P(('dp', 'fsdp')), may hold values from -0.21875 to 0.21875
- query_bias: bfloat16 [768], P(('dp', 'fsdp')), may hold values from -3 to 3
- value_bias: bfloat16 [768], P(('dp', 'fsdp')), may hold values from -3 to 3
- rel_table: bfloat16 [8800], P(('dp', 'fsdp')), may hold values from -4 to 4
- out_weight: bfloat16 [589824], P(('dp', 'fsdp')), may hold values from -1.25 to 1.25
- out_bias: bfloat16 [768], P(('dp', 'fsdp')), may hold values from -3 to 3
- attn_scale: bfloat16 [768], P(('dp', 'fsdp')), may hold values from 0.099609375 to 1.8984375
- post_gain: bfloat16 [768], P(('dp', 'fsdp')), may hold values from 0.099609375 to 1.8984375
- post_shift: bfloat16 [768], P(('dp', 'fsdp')), may hold values from -3 to 3
- up_weight: bfloat16 [2359296], P(('dp', 'fsdp')), may hold values from -0.21875 to 0.21875
- up_bias: bfloat16 [3072], P(('dp', 'fsdp')), may hold values from -3 to 3
- down_weight: bfloat16 [2359296], P(('dp', 'fsdp')), may hold values from -0.109375 to 0.109375
- down_bias: bfloat16 [768], P(('dp', 'fsdp')), may hold values from -3 to 3
- mlp_scale: bfloat16 [768], P(('dp', 'fsdp')), may hold values from 0.099609375 to 1.8984375
Outputs:
- layer_out: bfloat16 [160, 197, 768], P(('dp', 'fsdp'))
- patch_grad: bfloat16 [160, 197, 768], P(('dp', 'fsdp'))
- mask_token_grad: float32 [768], P(('dp', 'fsdp'))
- pre_gain_grad: float32 [768], P(('dp', 'fsdp'))
- pre_shift_grad: float32 [768], P(('dp', 'fsdp'))
- qkv_weight_grad: float32 [1769472], P(('dp', 'fsdp'))
- query_bias_grad: float32 [768], P(('dp', 'fsdp'))
- value_bias_grad: float32 [768], P(('dp', 'fsdp'))
- rel_table_grad: float32 [8800], P(('dp', 'fsdp'))
- out_weight_grad: float32 [589824], P(('dp', 'fsdp'))
- out_bias_grad: float32 [768], P(('dp', 'fsdp'))
- attn_scale_grad: float32 [768], P(('dp', 'fsdp'))
- post_gain_grad: float32 [768], P(('dp', 'fsdp'))
- post_shift_grad: float32 [768], P(('dp', 'fsdp'))
- up_weight_grad: float32 [2359296], P(('dp', 'fsdp'))
- up_bias_grad: float32 [3072], P(('dp', 'fsdp'))
- down_weight_grad: float32 [2359296], P(('dp', 'fsdp'))
- down_bias_grad: float32 [768], P(('dp', 'fsdp'))
- mlp_scale_grad: float32 [768], P(('dp', 'fsdp'))
The draws below stay inside these ranges and needn't reach their ends.
Inputs may be any that keep to these rules, and one draw needn't show every extreme that they name: `patch_mask`: row 0 (the class token) of every image is 0 and every image has at least one masked patch.
All inputs are finite; a program needn't handle non-finite values.
Results may differ from the reference program's by a relative error of at most 0.012.
Values may be sent and summed in bfloat16 or wider, within the bound.
A program may use at most 192 MiB of HBM per device.

```python
import math
import jax
import jax.numpy as jnp
from jax import lax

D = 768
HEADS = 12
FF = 3072
GRID = 14
IMG_DEV = 5
SEQ = 197
NREL = 732
IMAGES = 160
P_VEC = 768
P_HID = 3072
P_QKV = 1769472
P_PROJ = 589824
P_MLP = 2359296
P_TAB = 8800


def draw_patch_mask(key, part):
    patch_count = SEQ - 1
    first_key, second_key = jax.random.split(jax.random.fold_in(key, 7))
    exponent = jax.random.randint(first_key, (IMAGES,), 0, 7)
    masked_count = jnp.maximum(1, patch_count * 2 ** exponent // 64)
    raw_scores = jax.random.randint(second_key, (IMAGES, patch_count), 0, 2 ** 20)
    distinct = raw_scores * patch_count + jnp.arange(patch_count, dtype=jnp.int32)[None, :]
    order = jnp.argsort(distinct, axis=1)
    ranking = jnp.argsort(order, axis=1)
    chosen = (ranking < masked_count[:, None]).astype(jnp.int32)
    class_col = jnp.zeros((IMAGES, 1), jnp.int32)
    return jnp.concatenate([class_col, chosen], axis=1).astype(jnp.int32)


def level_of(key, dims, shards, low, largest):
    loudness, own = 1.0, jax.random.fold_in(key, 6)
    for dim, shards_of in shards:
        steps = jnp.exp(jax.random.uniform(jax.random.fold_in(own, dim), (shards_of,), jnp.float32, low / len(shards), largest / len(shards)))
        loudness = loudness * jnp.repeat(steps, dims[dim] // shards_of).reshape([-1 if axis == dim else 1 for axis in range(len(dims))])
    return loudness


def normal_values(own_key, extent, deviation, reach, cuts=(), kind=jnp.bfloat16):
    drawn = jax.random.normal(own_key, extent, jnp.float32) * deviation
    if len(cuts) > 0:
        drawn = level_of(own_key, extent, cuts, -0.22, 0.18) * drawn
    return jnp.clip(drawn, min=-reach, max=reach).astype(kind)


def setup_inputs(seed: int = 0) -> dict:
    arg_keys = jax.random.split(jax.random.key(seed), 21)
    return {
        "patches": normal_values(arg_keys[0], (IMAGES, SEQ, D), 1.0, 6.0, ((0, 32),)),
        "patch_mask": draw_patch_mask(jax.random.fold_in(arg_keys[20], 71), 0),
        "cotangent": normal_values(arg_keys[2], (IMAGES, SEQ, D), 1.0, 6.0, ((0, 32),)),
        "mask_token": normal_values(arg_keys[3], (P_VEC,), 1.0, 5.0, ((0, 32),)),
        "pre_gain": jnp.clip(1.0 + 0.18 * jax.random.normal(arg_keys[4], (P_VEC,), jnp.float32), 0.099609375, 1.8984375).astype(jnp.bfloat16),
        "pre_shift": normal_values(arg_keys[5], (P_VEC,), 0.5, 3.0, ((0, 32),)),
        "qkv_weight": normal_values(arg_keys[6], (P_QKV,), D ** -0.5, 0.21875, ((0, 32),)),
        "query_bias": normal_values(arg_keys[7], (P_VEC,), 0.5, 3.0, ((0, 32),)),
        "value_bias": normal_values(arg_keys[8], (P_VEC,), 0.5, 3.0, ((0, 32),)),
        "rel_table": normal_values(arg_keys[9], (P_TAB,), 1.0, 4.0, ((0, 32),)),
        "out_weight": normal_values(arg_keys[10], (P_PROJ,), (D // 32) ** -0.5, 1.25, ((0, 32),)),
        "out_bias": normal_values(arg_keys[11], (P_VEC,), 0.5, 3.0, ((0, 32),)),
        "attn_scale": jnp.clip(1.0 + 0.18 * jax.random.normal(arg_keys[12], (P_VEC,), jnp.float32), 0.099609375, 1.8984375).astype(jnp.bfloat16),
        "post_gain": jnp.clip(1.0 + 0.18 * jax.random.normal(arg_keys[13], (P_VEC,), jnp.float32), 0.099609375, 1.8984375).astype(jnp.bfloat16),
        "post_shift": normal_values(arg_keys[14], (P_VEC,), 0.5, 3.0, ((0, 32),)),
        "up_weight": normal_values(arg_keys[15], (P_MLP,), D ** -0.5, 0.21875, ((0, 32),)),
        "up_bias": normal_values(arg_keys[16], (P_HID,), 0.5, 3.0, ((0, 32),)),
        "down_weight": normal_values(arg_keys[17], (P_MLP,), FF ** -0.5, 0.109375, ((0, 32),)),
        "down_bias": normal_values(arg_keys[18], (P_VEC,), 0.5, 3.0, ((0, 32),)),
        "mlp_scale": jnp.clip(1.0 + 0.18 * jax.random.normal(arg_keys[19], (P_VEC,), jnp.float32), 0.099609375, 1.8984375).astype(jnp.bfloat16),
    }


norm_eps = 1e-06
precise = lax.Precision.HIGHEST

@jax.custom_vjp
def low(v):
    return lax.optimization_barrier(v.astype(jnp.bfloat16)).astype(jnp.float32)

@jax.custom_vjp
def low_back(v):
    return v

def low_keep(v):
    return (low(v), None)

def low_pass(kept, grad):
    return (grad,)

def back_keep(v):
    return (v, None)

def back_low(kept, grad):
    return (low(grad),)
low.defvjp(low_keep, low_pass)
low_back.defvjp(back_keep, back_low)

def relative_index(row_ids, col_ids, grid_side):
    table_rows = (2 * grid_side - 1) ** 2 + 3
    rel_rows = row_ids - 1
    rel_cols = col_ids - 1
    down_diff = rel_rows // grid_side - rel_cols // grid_side + grid_side - 1
    across_diff = rel_rows % grid_side - rel_cols % grid_side + grid_side - 1
    inside = down_diff * (2 * grid_side - 1) + across_diff
    first_row = row_ids == 0
    first_col = col_ids == 0
    position = jnp.where(first_row, table_rows - 3, jnp.where(first_col, table_rows - 2, inside))
    position = jnp.where(first_row & first_col, table_rows - 1, position)
    return position.astype(jnp.int32)

def unpack(flat, shape):
    entries = math.prod(shape)
    return flat[:entries].reshape(shape)

def layer_norm(values, gain, shift):
    average = lax.optimization_barrier(jnp.mean(values, axis=-1, keepdims=True))
    centred = values - average
    variance = lax.optimization_barrier(jnp.mean(centred * centred, axis=-1, keepdims=True))
    return centred * lax.rsqrt(variance + norm_eps) * gain + shift

def matmul(left, right):
    return jnp.dot(left, right, precision=precise, preferred_element_type=jnp.float32)

def block_forward(tokens, mask_rows, params, pos_bias):
    mask_token, pre_gain, pre_shift, qkv_weight, query_bias, value_bias, out_weight, out_bias, attn_scale, post_gain, post_shift, up_weight, up_bias, down_weight, down_bias, mlp_scale = params
    images, seq_len, model_dim = tokens.shape
    four_dims = (images, seq_len, HEADS, model_dim // HEADS)
    initial = jnp.where(mask_rows[..., None] == 1, mask_token, tokens).reshape(-1, model_dim)
    normed_pre = low(layer_norm(initial, pre_gain, pre_shift))
    projected = low_back(matmul(normed_pre, qkv_weight))
    queries = low((projected[:, :model_dim] + query_bias) * 0.125).reshape(four_dims)
    keys_all = low(projected[:, model_dim:2 * model_dim]).reshape(four_dims)
    values_all = low(projected[:, 2 * model_dim:] + value_bias).reshape(four_dims)
    scores = low_back(jnp.einsum('ishd,ithd->ihst', queries, keys_all, precision=precise)) + pos_bias[None]
    probs = low(jax.nn.softmax(scores, axis=-1))
    attended = jnp.einsum('ihst,ithd->ishd', probs, values_all, precision=precise).reshape(-1, model_dim)
    attended = low(low_back(attended))
    branch = low_back(matmul(attended, out_weight)) + out_bias
    middle = initial + attn_scale * branch
    normed_post = low(layer_norm(middle, post_gain, post_shift))
    up_rows = low_back(matmul(normed_post, up_weight)) + up_bias
    hidden = low(jax.nn.gelu(up_rows, approximate=False))
    down_rows = low_back(matmul(hidden, down_weight)) + down_bias
    result = middle + mlp_scale * down_rows
    return result.reshape(images, seq_len, model_dim)

def reference(patches, patch_mask, cotangent, mask_token, pre_gain, pre_shift, qkv_weight, query_bias, value_bias, rel_table, out_weight, out_bias, attn_scale, post_gain, post_shift, up_weight, up_bias, down_weight, down_bias, mlp_scale):
    shapes = ((D,), (D,), (D,), (D, 3 * D), (D,), (D,), (NREL, HEADS), (D, D), (D,), (D,), (D,), (D,), (D, FF), (FF,), (FF, D), (D,), (D,))
    flats = (mask_token, pre_gain, pre_shift, qkv_weight, query_bias, value_bias, rel_table, out_weight, out_bias, attn_scale, post_gain, post_shift, up_weight, up_bias, down_weight, down_bias, mlp_scale)
    flats_wide = tuple((flat.astype(jnp.float32) for flat in flats))
    tokens = patches.astype(jnp.float32)
    positions = jnp.arange(SEQ, dtype=jnp.int32)
    table_index = relative_index(positions[:, None], positions[None, :], GRID)
    mask_blocks = patch_mask.reshape(-1, IMG_DEV, SEQ)

    def forward(tokens_in, *flat_params):
        params = [unpack(flat, shape) for flat, shape in zip(flat_params, shapes)]
        table = params[6]
        pos_bias = jnp.transpose(table[table_index], (2, 0, 1))
        others = tuple(params[:6] + params[7:])
        token_blocks = tokens_in.reshape(-1, IMG_DEV, SEQ, D)

        def one_block(pair):
            return block_forward(pair[0], pair[1], others, pos_bias)
        outputs = lax.map(jax.checkpoint(one_block), (token_blocks, mask_blocks))
        return outputs.reshape(tokens_in.shape)
    layer_out, pullback = jax.vjp(forward, tokens, *flats_wide)
    seed_grad = cotangent.astype(jnp.float32) * patch_mask[..., None].astype(jnp.float32)
    grads = pullback(seed_grad)
    return (layer_out.astype(jnp.bfloat16), grads[0].astype(jnp.bfloat16), grads[1], grads[2], grads[3], grads[4], grads[5], grads[6], grads[7], grads[8], grads[9], grads[10], grads[11], grads[12], grads[13], grads[14], grads[15], grads[16], grads[17])
```

```python
import functools
import math

import jax
import jax.numpy as jnp
from jax import lax
from jax.experimental import pallas as pl
from jax.experimental.pallas import tpu as pltpu
from jax.sharding import PartitionSpec as P

HEADS = 12
FF = 3072
GRID = 14
MESH_IDS = pl.DeviceIdType.MESH
ANY = pl.BlockSpec(memory_space=pl.ANY)
VMEM = pl.BlockSpec(memory_space=pltpu.VMEM)
LIMIT = 60 << 20


class Place:
    def __init__(self, sizes):
        self.Y, self.A, self.B = sizes
        self.y = lax.axis_index("dp")
        f = lax.axis_index("fsdp")
        self.c = f % 2
        self.b = (f // 2) % self.B
        self.a = f // (2 * self.B)

    def dev(self, y=None, a=None, b=None, c=None):
        y = self.y if y is None else y
        a = self.a if a is None else a
        b = self.b if b is None else b
        c = self.c if c is None else c
        return (y, (a * self.B + b) * 2 + c)

    def barrier(self):
        sem = pltpu.get_barrier_semaphore()
        peers = [self.dev(c=1 - self.c)]
        peers += [self.dev(a=(self.a + j) % self.A) for j in range(1, self.A)]
        peers += [self.dev(b=(self.b + j) % self.B) for j in range(1, self.B)]
        peers += [self.dev(y=(self.y + j) % self.Y) for j in range(1, self.Y)]
        for peer in peers:
            pl.semaphore_signal(sem, inc=1, device_id=peer, device_id_type=MESH_IDS)
        pl.semaphore_wait(sem, len(peers))

    def both(self, body):
        @pl.when(self.c == 0)
        def _():
            body(0)

        @pl.when(self.c == 1)
        def _():
            body(1)


def remote(src, dst, send, recv, dev):
    return pltpu.make_async_remote_copy(
        src_ref=src, dst_ref=dst, send_sem=send, recv_sem=recv, device_id=dev, device_id_type=MESH_IDS
    )


class Gather:
    @staticmethod
    def sems(sizes):
        Y, A, B = sizes
        n = (A - 1) + (Y * B - 1) + Y * B
        return [pltpu.SemaphoreType.DMA((n,)), pltpu.SemaphoreType.DMA((n,)), pltpu.SemaphoreType.DMA((1,))]

    def __init__(self, place, shard, full, send, recv, local):
        self.p, self.shard, self.full = place, shard, full
        self.send, self.recv, self.local = send, recv, local

    def own(self, a=None):
        p = self.p
        a = p.a if a is None else a
        return self.full.at[p.y * p.A + a, p.b, p.c]

    def unit(self, ry, rb, c):
        p = self.p
        yy = (p.y + ry) % p.Y
        bb = (p.b + rb) % p.B
        return self.full.at[pl.ds(yy * p.A, p.A), bb, c]

    def local_copy(self):
        return pltpu.make_async_copy(self.shard, self.own(), self.local.at[0])

    def a_copy(self, j, sender):
        p = self.p
        dst = self.own() if sender else self.own((p.a - j) % p.A)
        i = j - 1
        return remote(self.shard, dst, self.send.at[i], self.recv.at[i], p.dev(a=(p.a + j) % p.A))

    def unit_copy(self, core, stage, j, u, sender):
        p = self.p
        n1, n2 = (p.B, p.Y) if core == 0 else (p.Y, p.B)
        if stage == 1:
            i = j - 1
            first, second = (0 if sender else -j), 0
        else:
            i = (n1 - 1) + (j - 1) * n1 + u
            first, second = u, (0 if sender else -j)
        ry, rb = (second, first) if core == 0 else (first, second)
        digit_b = (core == 0) == (stage == 1)
        dev = p.dev(b=(p.b + j) % p.B) if digit_b else p.dev(y=(p.y + j) % p.Y)
        ref = self.unit(ry % p.Y, rb % p.B, p.c)
        i += p.A - 1
        return remote(ref, ref, self.send.at[i], self.recv.at[i], dev), (ry % p.Y, rb % p.B)

    def twin_copy(self, ry, rb, sender):
        p = self.p
        i = (p.A - 1) + (p.Y * p.B - 1) + ry * p.B + rb
        ref = self.unit(ry, rb, p.c if sender else 1 - p.c)
        return remote(ref, ref, self.send.at[i], self.recv.at[i], p.dev(c=1 - p.c))

    def start(self):
        self.local_copy().start()
        for j in range(1, self.p.A):
            self.a_copy(j, True).start()

    def step1(self):
        p = self.p
        self.local_copy().wait()
        for j in range(1, p.A):
            self.a_copy(j, False).wait_recv()

        def body(core):
            n1 = p.B if core == 0 else p.Y
            for j in range(1, n1):
                self.unit_copy(core, 1, j, 0, True)[0].start()

        p.both(body)
        self.twin_copy(0, 0, True).start()

    def step2(self):
        p = self.p

        def body(core):
            n1, n2 = (p.B, p.Y) if core == 0 else (p.Y, p.B)
            arrived = []
            for j in range(1, n1):
                copy, unit = self.unit_copy(core, 1, j, 0, False)
                copy.wait_recv()
                arrived.append(unit)
            for u in range(n1):
                for j in range(1, n2):
                    self.unit_copy(core, 2, j, u, True)[0].start()
            for unit in arrived:
                self.twin_copy(*unit, True).start()

        p.both(body)

    def step3(self):
        p = self.p

        def body(core):
            n1, n2 = (p.B, p.Y) if core == 0 else (p.Y, p.B)
            for u in range(n1):
                for j in range(1, n2):
                    copy, unit = self.unit_copy(core, 2, j, u, False)
                    copy.wait_recv()
                    self.twin_copy(*unit, True).start()

        p.both(body)

    def finish(self):
        p = self.p
        for ry in range(p.Y):
            for rb in range(p.B):
                self.twin_copy(ry, rb, False).wait_recv()
                self.twin_copy(ry, rb, True).wait_send()
        for j in range(1, p.A):
            self.a_copy(j, True).wait_send()

        def body(core):
            n1, n2 = (p.B, p.Y) if core == 0 else (p.Y, p.B)
            for j in range(1, n1):
                self.unit_copy(core, 1, j, 0, True)[0].wait_send()
            for u in range(n1):
                for j in range(1, n2):
                    self.unit_copy(core, 2, j, u, True)[0].wait_send()

        p.both(body)


class Reduce:
    @staticmethod
    def slots(sizes):
        Y, A, B = sizes
        return max((Y - 1) * B, (B - 1) * Y)

    @staticmethod
    def scratch(sizes, r, c, dtype):
        Y, A, B = sizes
        n = 1 + Y * B - 1 + (A - 1)
        return [
            pltpu.VMEM((Y * A, B, r, c), dtype),
            pltpu.VMEM((Y * A, B, r, c), dtype),
            pltpu.VMEM((Reduce.slots(sizes) * A, r, c), dtype),
            pltpu.VMEM((max(Y - 1, B - 1) * A, r, c), dtype),
            pltpu.VMEM((A - 1, r, c), dtype),
            pltpu.SemaphoreType.DMA((n,)),
            pltpu.SemaphoreType.DMA((n,)),
            pltpu.SemaphoreType.DMA((1,)),
        ]

    def __init__(self, place, partial, out, own, land1, land2, land3, land4, send, recv, local):
        self.p, self.partial, self.out = place, partial, out
        self.own, self.land1, self.land2, self.land3, self.land4 = own, land1, land2, land3, land4
        self.send, self.recv, self.local = send, recv, local

    def twin(self):
        p = self.p
        return remote(
            self.partial.at[:, :, 1 - p.c], self.land1, self.send.at[0], self.recv.at[0], p.dev(c=1 - p.c)
        )

    def local_copy(self):
        return pltpu.make_async_copy(self.partial.at[:, :, self.p.c], self.own, self.local.at[0])

    def order(self, core):
        p = self.p
        return (p.Y, p.B) if core == 0 else (p.B, p.Y)

    def rel(self, core, first, second):
        p = self.p
        ry, rb = (first, second) if core == 0 else (second, first)
        return (p.y + ry) % p.Y, (p.b + rb) % p.B

    def peer(self, core, stage, j):
        p = self.p
        if (core == 0) == (stage == 1):
            return p.dev(y=(p.y + j) % p.Y)
        return p.dev(b=(p.b + j) % p.B)

    def copy1(self, core, j, u):
        p = self.p
        n1, n2 = self.order(core)
        yy, bb = self.rel(core, j, u)
        slot = (j - 1) * n2 + u
        i = 1 + slot
        return remote(
            self.own.at[pl.ds(yy * p.A, p.A), bb],
            self.land2.at[pl.ds(slot * p.A, p.A)],
            self.send.at[i],
            self.recv.at[i],
            self.peer(core, 1, j),
        )

    def copy2(self, core, j):
        p = self.p
        n1, n2 = self.order(core)
        yy, bb = self.rel(core, 0, j)
        i = 1 + (n1 - 1) * n2 + (j - 1)
        return remote(
            self.own.at[pl.ds(yy * p.A, p.A), bb],
            self.land3.at[pl.ds((j - 1) * p.A, p.A)],
            self.send.at[i],
            self.recv.at[i],
            self.peer(core, 2, j),
        )

    def copy3(self, j):
        p = self.p
        i = 1 + p.Y * p.B - 1 + (j - 1)
        a = (p.a + j) % p.A
        return remote(
            self.own.at[p.y * p.A + a, p.b], self.land4.at[j - 1], self.send.at[i], self.recv.at[i], p.dev(a=a)
        )

    def start(self):
        self.twin().start()
        self.local_copy().start()

    def step1(self):
        p = self.p
        self.local_copy().wait()
        self.twin().wait_recv()

        def add(i, _):
            for b in range(p.B):
                total = self.own[i, b].astype(jnp.float32) + self.land1[i, b].astype(jnp.float32)
                self.own[i, b] = total.astype(self.own.dtype)
            return 0

        lax.fori_loop(0, p.Y * p.A, add, 0)

        def body(core):
            n1, n2 = self.order(core)
            for j in range(1, n1):
                for u in range(n2):
                    self.copy1(core, j, u).start()

        p.both(body)

    def step2(self):
        p = self.p

        def body(core):
            n1, n2 = self.order(core)
            for j in range(1, n1):
                for u in range(n2):
                    self.copy1(core, j, u).wait_recv()
            for u in range(n2):
                yy, bb = self.rel(core, 0, u)

                def add(i, _):
                    total = self.own[yy * p.A + i, bb].astype(jnp.float32)
                    for j in range(1, n1):
                        total += self.land2[((j - 1) * n2 + u) * p.A + i].astype(jnp.float32)
                    self.own[yy * p.A + i, bb] = total.astype(self.own.dtype)
                    return 0

                lax.fori_loop(0, p.A, add, 0)
            for j in range(1, n2):
                self.copy2(core, j).start()

        p.both(body)

    def step3(self):
        p = self.p

        def body(core):
            n1, n2 = self.order(core)
            for j in range(1, n2):
                self.copy2(core, j).wait_recv()

            def add(i, _):
                total = self.own[p.y * p.A + i, p.b].astype(jnp.float32)
                for j in range(1, n2):
                    total += self.land3[(j - 1) * p.A + i].astype(jnp.float32)
                self.own[p.y * p.A + i, p.b] = total.astype(self.own.dtype)
                return 0

            lax.fori_loop(0, p.A, add, 0)

        p.both(body)
        for j in range(1, p.A):
            self.copy3(j).start()

    def finish(self):
        p = self.p
        total = self.own[p.y * p.A + p.a, p.b].astype(jnp.float32)
        for j in range(1, p.A):
            self.copy3(j).wait_recv()
            total += self.land4[j - 1].astype(jnp.float32)
        self.out[...] = total
        self.twin().wait_send()
        for j in range(1, p.A):
            self.copy3(j).wait_send()

        def body(core):
            n1, n2 = self.order(core)
            for j in range(1, n1):
                for u in range(n2):
                    self.copy1(core, j, u).wait_send()
            for j in range(1, n2):
                self.copy2(core, j).wait_send()

        p.both(body)


def gather_kernel(sizes, n, *refs):
    shards, fulls, sems = refs[:n], refs[n : 2 * n], refs[2 * n :]
    place = Place(sizes)
    place.barrier()
    gathers = [Gather(place, shards[k], fulls[k], *sems[3 * k : 3 * k + 3]) for k in range(n)]
    for g in gathers:
        g.start()
    for g in gathers:
        g.step1()
    for g in gathers:
        g.step2()
    for g in gathers:
        g.step3()
    for g in gathers:
        g.finish()


def gather_call(sizes, shards, collective_id):
    Y, A, B = sizes
    n = len(shards)
    shapes = [jax.ShapeDtypeStruct((Y * A, B, 2, *s.shape), s.dtype) for s in shards]
    return pl.pallas_call(
        functools.partial(gather_kernel, sizes, n),
        out_shape=shapes,
        in_specs=[ANY] * n,
        out_specs=[ANY] * n,
        scratch_shapes=[s for _ in range(n) for s in Gather.sems(sizes)],
        compiler_params=pltpu.CompilerParams(
            collective_id=collective_id, has_side_effects=True, vmem_limit_bytes=LIMIT
        ),
        name="gather",
    )(*shards)


def reduce_kernel(sizes, n, *refs):
    partials, outs, scratch = refs[:n], refs[n : 2 * n], refs[2 * n :]
    place = Place(sizes)
    place.barrier()
    sums = [Reduce(place, partials[k], outs[k], *scratch[8 * k : 8 * k + 8]) for k in range(n)]
    for s in sums:
        s.start()
    for s in sums:
        s.step1()
    for s in sums:
        s.step2()
    for s in sums:
        s.step3()
    for s in sums:
        s.finish()


def reduce_call(sizes, partials, collective_id):
    Y, A, B = sizes
    n = len(partials)
    partials = [x.reshape(Y * A, B, 2, *x.shape[1:]) for x in partials]
    shapes = [jax.ShapeDtypeStruct(x.shape[3:], jnp.float32) for x in partials]
    return pl.pallas_call(
        functools.partial(reduce_kernel, sizes, n),
        out_shape=shapes,
        in_specs=[ANY] * n,
        out_specs=[VMEM] * n,
        scratch_shapes=[
            s for x in partials for s in Reduce.scratch(sizes, x.shape[3], x.shape[4], x.dtype)
        ],
        compiler_params=pltpu.CompilerParams(
            collective_id=collective_id, has_side_effects=True, vmem_limit_bytes=LIMIT
        ),
        name="reduce",
    )(*partials)


def mesh_sizes(dp, fsdp):
    chips = fsdp // 2
    across = math.gcd(chips, 4)
    return (dp, across, chips // across)


def block_shape(entries, width):
    rows = entries // width
    return (rows, width) if rows % 8 == 0 else (entries // 128, 128)


TILE = 16


def pack_small(vectors, hidden, table):
    lanes = 128
    rows = [jnp.pad(v, (0, lanes - v.shape[0])) for v in vectors]
    rows.append(jnp.pad(hidden, (0, lanes - hidden.shape[0])))
    table_rows = -(-table.shape[0] // lanes)
    rows.append(jnp.pad(table, (0, table_rows * lanes - table.shape[0])))
    flat = jnp.concatenate(rows)
    return jnp.pad(flat, (0, TILE * lanes - flat.shape[0])).reshape(TILE, lanes)


norm_eps = 1e-06
block_rows = 16


def relative_index(row_ids, col_ids, grid_side):
    table_rows = (2 * grid_side - 1) ** 2 + 3
    rel_rows = row_ids - 1
    rel_cols = col_ids - 1
    down_diff = rel_rows // grid_side - rel_cols // grid_side + grid_side - 1
    across_diff = rel_rows % grid_side - rel_cols % grid_side + grid_side - 1
    inside = down_diff * (2 * grid_side - 1) + across_diff
    first_row = row_ids == 0
    first_col = col_ids == 0
    position = jnp.where(first_row, table_rows - 3, jnp.where(first_col, table_rows - 2, inside))
    position = jnp.where(first_row & first_col, table_rows - 1, position)
    return position


def position_onehot(block_id, seq_len, grid_side, table_rows):
    row_ids = block_id * block_rows + jnp.arange(block_rows, dtype=jnp.int32)
    col_ids = jnp.arange(seq_len, dtype=jnp.int32)
    position = relative_index(row_ids[:, None], col_ids[None, :], grid_side)
    position = jnp.where(row_ids[:, None] < seq_len, position, -1)
    table_ids = jnp.arange(table_rows, dtype=jnp.int32)
    onehot = (position[:, :, None] == table_ids[None, None, :]).astype(jnp.bfloat16)
    return onehot.reshape(block_rows * seq_len, table_rows)


def unpack(flat, shape):
    entries = math.prod(shape)
    return flat[:entries].reshape(shape)


def pad_flat(values, length):
    flat = values.reshape(-1)
    return jnp.pad(flat, (0, length - flat.shape[0]))


def normalize(values):
    average = jnp.mean(values, axis=-1, keepdims=True)
    centred = values - average
    variance = jnp.mean(centred * centred, axis=-1, keepdims=True)
    inverse = lax.rsqrt(variance + norm_eps)
    return (centred * inverse, inverse)


def norm_back(grad_normed, normal, inverse, gain):
    scaled = grad_normed * gain
    first_mean = jnp.mean(scaled, axis=-1, keepdims=True)
    second_mean = jnp.mean(scaled * normal, axis=-1, keepdims=True)
    return inverse * (scaled - first_mean - normal * second_mean)


def gelu_slope(values):
    return (
        0.5 * (1.0 + lax.erf(values * 0.7071067811865476))
        + values * jnp.exp(-0.5 * values * values) * 0.3989422804014327
    )


def per_device(
    patches,
    patch_mask,
    cotangent,
    mask_token,
    pre_gain,
    pre_shift,
    qkv_weight,
    query_bias,
    value_bias,
    rel_table,
    out_weight,
    out_bias,
    attn_scale,
    post_gain,
    post_shift,
    up_weight,
    up_bias,
    down_weight,
    down_bias,
    mlp_scale,
):
    images, seq_len, model_dim = patches.shape
    heads = HEADS
    head_dim = model_dim // heads
    hidden_dim = FF
    grid_side = GRID
    table_rows = (2 * GRID - 1) ** 2 + 3
    block_count = -(-seq_len // block_rows)
    padded_rows = block_count * block_rows
    four_dims = (images, seq_len, heads, head_dim)
    total_devices = lax.axis_size(("dp", "fsdp"))
    sizes = mesh_sizes(lax.axis_size("dp"), lax.axis_size("fsdp"))
    vec_shards = (
        mask_token, pre_gain, pre_shift, query_bias, value_bias, out_bias, attn_scale,
        post_gain, post_shift, down_bias, mlp_scale,
    )
    small = pack_small(vec_shards, up_bias, rel_table)
    widths = (3 * model_dim, model_dim, hidden_dim, model_dim)
    mats = (qkv_weight, out_weight, up_weight, down_weight)
    blocks = [m.reshape(block_shape(m.shape[0], w)) for m, w in zip(mats, widths)]
    small_full, *mats_full = gather_call(sizes, [small] + blocks, 0)
    qkv_w, out_w, up_w, down_w = [m.reshape(-1, w) for m, w in zip(mats_full, widths)]
    rows_full = small_full.reshape(total_devices, TILE, 128)
    per_vec = mask_token.shape[0]
    vectors = [rows_full[:, i, :per_vec].reshape(-1).astype(jnp.float32) for i in range(11)]
    (
        token_fill, pre_g, pre_s, query_b, value_b, out_b, attn_g, post_g, post_s, down_b, mlp_g,
    ) = vectors
    up_b = rows_full[:, 11, : up_bias.shape[0]].reshape(-1).astype(jnp.float32)
    table = rows_full[:, 12:].reshape(total_devices, -1)[:, : rel_table.shape[0]].reshape(-1)
    table = table[: table_rows * heads].reshape(table_rows, heads)
    masked = patch_mask.reshape(-1, 1) == 1
    token_rows = patches.reshape(-1, model_dim).astype(jnp.float32)
    initial = jnp.where(masked, token_fill[None, :], token_rows)
    normal_pre, inverse_pre = normalize(initial)
    normed_pre = (normal_pre * pre_g + pre_s).astype(jnp.bfloat16)
    projected = jnp.dot(normed_pre, qkv_w, preferred_element_type=jnp.float32)
    queries = ((projected[:, :model_dim] + query_b) * 0.125).astype(jnp.bfloat16).reshape(four_dims)
    keys_all = projected[:, model_dim : 2 * model_dim].astype(jnp.bfloat16).reshape(four_dims)
    values_all = (projected[:, 2 * model_dim :] + value_b).astype(jnp.bfloat16).reshape(four_dims)

    def bias_rows(block_id):
        onehot = position_onehot(block_id, seq_len, grid_side, table_rows)
        return jnp.einsum("rh,ar->ha", table, onehot, preferred_element_type=jnp.float32)

    bias_pieces = lax.map(bias_rows, jnp.arange(block_count, dtype=jnp.int32))
    bias_pieces = bias_pieces.reshape(block_count, heads, block_rows, seq_len)
    pos_bias = jnp.transpose(bias_pieces, (1, 0, 2, 3)).reshape(heads, padded_rows, seq_len)[
        :, :seq_len
    ]
    scores = (
        jnp.einsum("ishd,ithd->ihst", queries, keys_all, preferred_element_type=jnp.float32)
        + pos_bias[None]
    )
    peak = jnp.max(scores, axis=-1, keepdims=True)
    shifted = jnp.exp(scores - peak)
    totals = jnp.sum(shifted, axis=-1, keepdims=True)
    probs = shifted / totals
    log_total = peak + jnp.log(totals)
    attended = jnp.einsum(
        "ihst,ithd->ishd",
        probs.astype(jnp.bfloat16),
        values_all,
        preferred_element_type=jnp.float32,
    )
    attended = attended.reshape(-1, model_dim).astype(jnp.bfloat16)
    branch = jnp.dot(attended, out_w, preferred_element_type=jnp.float32) + out_b
    middle = initial + attn_g * branch
    normal_post, inverse_post = normalize(middle)
    normed_post = (normal_post * post_g + post_s).astype(jnp.bfloat16)
    up_rows = jnp.dot(normed_post, up_w, preferred_element_type=jnp.float32) + up_b
    hidden = jax.nn.gelu(up_rows, approximate=False).astype(jnp.bfloat16)
    down_rows = jnp.dot(hidden, down_w, preferred_element_type=jnp.float32) + down_b
    result = middle + mlp_g * down_rows
    layer_out = result.astype(jnp.bfloat16).reshape(patches.shape)
    grad_out = cotangent.reshape(-1, model_dim).astype(jnp.float32) * masked.astype(jnp.float32)
    mlp_scale_grad = jnp.sum(grad_out * down_rows, axis=0)
    grad_down_rows = mlp_g * grad_out
    down_bias_grad = jnp.sum(grad_down_rows, axis=0)
    grad_down = grad_down_rows.astype(jnp.bfloat16)
    down_weight_grad = jnp.einsum(
        "ra,rb->ab", hidden, grad_down, preferred_element_type=jnp.float32
    )
    grad_hidden = jnp.einsum("rb,ab->ra", grad_down, down_w, preferred_element_type=jnp.float32)
    grad_up_rows = grad_hidden * gelu_slope(up_rows)
    up_bias_grad = jnp.sum(grad_up_rows, axis=0)
    grad_up = grad_up_rows.astype(jnp.bfloat16)
    up_weight_grad = jnp.einsum(
        "ra,rb->ab", normed_post, grad_up, preferred_element_type=jnp.float32
    )
    grad_normed_post = jnp.einsum("rb,ab->ra", grad_up, up_w, preferred_element_type=jnp.float32)
    post_gain_grad = jnp.sum(grad_normed_post * normal_post, axis=0)
    post_shift_grad = jnp.sum(grad_normed_post, axis=0)
    grad_middle = grad_out + norm_back(grad_normed_post, normal_post, inverse_post, post_g)
    attn_scale_grad = jnp.sum(grad_middle * branch, axis=0)
    grad_branch_rows = attn_g * grad_middle
    out_bias_grad = jnp.sum(grad_branch_rows, axis=0)
    grad_branch = grad_branch_rows.astype(jnp.bfloat16)
    out_weight_grad = jnp.einsum(
        "ra,rb->ab", attended, grad_branch, preferred_element_type=jnp.float32
    )
    grad_attended = jnp.einsum("rb,ab->ra", grad_branch, out_w, preferred_element_type=jnp.float32)
    grad_attended = grad_attended.astype(jnp.bfloat16).reshape(four_dims)
    scores_again = (
        jnp.einsum("ishd,ithd->ihst", queries, keys_all, preferred_element_type=jnp.float32)
        + pos_bias[None]
    )
    probs_again = jnp.exp(scores_again - log_total)
    grad_probs = jnp.einsum(
        "ishd,ithd->ihst", grad_attended, values_all, preferred_element_type=jnp.float32
    )
    grad_values = jnp.einsum(
        "ihst,ishd->ithd",
        probs_again.astype(jnp.bfloat16),
        grad_attended,
        preferred_element_type=jnp.float32,
    )
    inner_sum = jnp.sum(probs_again * grad_probs, axis=-1, keepdims=True)
    grad_scores = probs_again * (grad_probs - inner_sum)
    bias_grad = jnp.sum(grad_scores, axis=0)
    grad_scores_low = grad_scores.astype(jnp.bfloat16)
    grad_queries = (
        jnp.einsum("ihst,ithd->ishd", grad_scores_low, keys_all, preferred_element_type=jnp.float32)
        * 0.125
    )
    grad_keys = jnp.einsum(
        "ihst,ishd->ithd", grad_scores_low, queries, preferred_element_type=jnp.float32
    )
    grad_queries = grad_queries.reshape(-1, model_dim)
    grad_keys = grad_keys.reshape(-1, model_dim)
    grad_values = grad_values.reshape(-1, model_dim)
    query_bias_grad = jnp.sum(grad_queries, axis=0)
    value_bias_grad = jnp.sum(grad_values, axis=0)
    grad_projected = jnp.concatenate([grad_queries, grad_keys, grad_values], axis=1).astype(
        jnp.bfloat16
    )
    qkv_weight_grad = jnp.einsum(
        "ra,rb->ab", normed_pre, grad_projected, preferred_element_type=jnp.float32
    )
    grad_normed_pre = jnp.einsum(
        "rb,ab->ra", grad_projected, qkv_w, preferred_element_type=jnp.float32
    )
    pre_gain_grad = jnp.sum(grad_normed_pre * normal_pre, axis=0)
    pre_shift_grad = jnp.sum(grad_normed_pre, axis=0)
    grad_initial = grad_middle + norm_back(grad_normed_pre, normal_pre, inverse_pre, pre_g)
    mask_token_grad = jnp.sum(jnp.where(masked, grad_initial, 0.0), axis=0)
    patch_grad = jnp.where(masked, 0.0, grad_initial).astype(jnp.bfloat16).reshape(patches.shape)
    bias_grid = jnp.pad(bias_grad, ((0, 0), (0, padded_rows - seq_len), (0, 0)))
    bias_grid = bias_grid.reshape(heads, block_count, block_rows * seq_len)
    bias_grid = jnp.transpose(bias_grid, (1, 0, 2))

    def add_block(running, inputs):
        block_id, piece = inputs
        onehot = position_onehot(block_id, seq_len, grid_side, table_rows)
        upper = piece.astype(jnp.bfloat16)
        lower = (piece - upper.astype(jnp.float32)).astype(jnp.bfloat16)
        running = running + jnp.dot(upper, onehot, preferred_element_type=jnp.float32)
        running = running + jnp.dot(lower, onehot, preferred_element_type=jnp.float32)
        return (running, None)

    table_grad_t, _ = lax.scan(
        add_block,
        jnp.zeros((heads, table_rows), jnp.float32),
        (jnp.arange(block_count, dtype=jnp.int32), bias_grid),
    )
    table_grad = jnp.transpose(table_grad_t)
    vec_grads = (
        mask_token_grad, pre_gain_grad, pre_shift_grad, query_bias_grad, value_bias_grad,
        out_bias_grad, attn_scale_grad, post_gain_grad, post_shift_grad, down_bias_grad,
        mlp_scale_grad,
    )
    table_flat = pad_flat(table_grad, rel_table.shape[0] * total_devices)

    def lanes(value, count):
        value = value.reshape(total_devices, -1)
        return jnp.pad(value, ((0, 0), (0, count - value.shape[1])))

    small_grad = jnp.concatenate(
        [lanes(v, 128) for v in vec_grads]
        + [lanes(up_bias_grad, 128), lanes(table_flat, (TILE - 12) * 128)],
        axis=1,
    ).reshape(total_devices, TILE, 128)
    mat_grads = (qkv_weight_grad, out_weight_grad, up_weight_grad, down_weight_grad)
    partials = [
        g.astype(jnp.bfloat16).reshape(total_devices, *b.shape) for g, b in zip(mat_grads, blocks)
    ]
    *mat_own, small_own = reduce_call(sizes, partials + [small_grad], 1)
    qkv_o, out_o, up_o, down_o = [m.reshape(-1) for m in mat_own]
    vec_o = [small_own[i, :per_vec] for i in range(11)]
    up_bias_o = small_own[11, : up_bias.shape[0]]
    table_o = small_own[12:].reshape(-1)[: rel_table.shape[0]]
    (
        token_o, pre_gain_o, pre_shift_o, query_bias_o, value_bias_o, out_bias_o, attn_scale_o,
        post_gain_o, post_shift_o, down_bias_o, mlp_scale_o,
    ) = vec_o
    return (
        layer_out, patch_grad, token_o, pre_gain_o, pre_shift_o, qkv_o, query_bias_o, value_bias_o,
        table_o, out_o, out_bias_o, attn_scale_o, post_gain_o, post_shift_o, up_o, up_bias_o,
        down_o, down_bias_o, mlp_scale_o,
    )


def solution(mesh):
    in_specs = (
        P(("dp", "fsdp"), None, None),
        P(("dp", "fsdp"), None),
        P(("dp", "fsdp"), None, None),
        P(("dp", "fsdp")),
        P(("dp", "fsdp")),
        P(("dp", "fsdp")),
        P(("dp", "fsdp")),
        P(("dp", "fsdp")),
        P(("dp", "fsdp")),
        P(("dp", "fsdp")),
        P(("dp", "fsdp")),
        P(("dp", "fsdp")),
        P(("dp", "fsdp")),
        P(("dp", "fsdp")),
        P(("dp", "fsdp")),
        P(("dp", "fsdp")),
        P(("dp", "fsdp")),
        P(("dp", "fsdp")),
        P(("dp", "fsdp")),
        P(("dp", "fsdp")),
    )
    out_specs = (
        P(("dp", "fsdp"), None, None),
        P(("dp", "fsdp"), None, None),
        P(("dp", "fsdp")),
        P(("dp", "fsdp")),
        P(("dp", "fsdp")),
        P(("dp", "fsdp")),
        P(("dp", "fsdp")),
        P(("dp", "fsdp")),
        P(("dp", "fsdp")),
        P(("dp", "fsdp")),
        P(("dp", "fsdp")),
        P(("dp", "fsdp")),
        P(("dp", "fsdp")),
        P(("dp", "fsdp")),
        P(("dp", "fsdp")),
        P(("dp", "fsdp")),
        P(("dp", "fsdp")),
        P(("dp", "fsdp")),
        P(("dp", "fsdp")),
    )
    return jax.shard_map(
        per_device, mesh=mesh, in_specs=in_specs, out_specs=out_specs, check_vma=False
    )
```

```python
import functools
import math

import jax
import jax.numpy as jnp
from jax import lax
from jax.experimental import pallas as pl
from jax.experimental.pallas import tpu as pltpu
from jax.sharding import PartitionSpec as P

HEADS = 12
FF = 3072
GRID = 14
MESH_IDS = pl.DeviceIdType.MESH
ANY = pl.BlockSpec(memory_space=pl.ANY)
VMEM = pl.BlockSpec(memory_space=pltpu.VMEM)
LIMIT = 60 << 20


class Place:
    def __init__(self, sizes):
        self.Y, self.A, self.B = sizes
        self.y = lax.axis_index("dp")
        f = lax.axis_index("fsdp")
        self.c = f % 2
        self.b = (f // 2) % self.B
        self.a = f // (2 * self.B)

    def dev(self, y=None, a=None, b=None, c=None):
        y = self.y if y is None else y
        a = self.a if a is None else a
        b = self.b if b is None else b
        c = self.c if c is None else c
        return (y, (a * self.B + b) * 2 + c)

    def barrier(self):
        sem = pltpu.get_barrier_semaphore()
        peers = [self.dev(c=1 - self.c)]
        peers += [self.dev(a=(self.a + j) % self.A) for j in range(1, self.A)]
        peers += [self.dev(b=(self.b + j) % self.B) for j in range(1, self.B)]
        peers += [self.dev(y=(self.y + j) % self.Y) for j in range(1, self.Y)]
        for peer in peers:
            pl.semaphore_signal(sem, inc=1, device_id=peer, device_id_type=MESH_IDS)
        pl.semaphore_wait(sem, len(peers))

    def both(self, body):
        @pl.when(self.c == 0)
        def _():
            body(0)

        @pl.when(self.c == 1)
        def _():
            body(1)


def remote(src, dst, send, recv, dev):
    return pltpu.make_async_remote_copy(
        src_ref=src, dst_ref=dst, send_sem=send, recv_sem=recv, device_id=dev, device_id_type=MESH_IDS
    )


class Gather:
    @staticmethod
    def sems(sizes):
        Y, A, B = sizes
        n = (A - 1) + (Y * B - 1) + Y * B
        return [pltpu.SemaphoreType.DMA((n,)), pltpu.SemaphoreType.DMA((n,)), pltpu.SemaphoreType.DMA((1,))]

    def __init__(self, place, shard, full, send, recv, local):
        self.p, self.shard, self.full = place, shard, full
        self.send, self.recv, self.local = send, recv, local

    def own(self, a=None):
        p = self.p
        a = p.a if a is None else a
        return self.full.at[p.y * p.A + a, p.b, p.c]

    def unit(self, ry, rb, c):
        p = self.p
        yy = (p.y + ry) % p.Y
        bb = (p.b + rb) % p.B
        return self.full.at[pl.ds(yy * p.A, p.A), bb, c]

    def local_copy(self):
        return pltpu.make_async_copy(self.shard, self.own(), self.local.at[0])

    def a_copy(self, j, sender):
        p = self.p
        dst = self.own() if sender else self.own((p.a - j) % p.A)
        i = j - 1
        return remote(self.shard, dst, self.send.at[i], self.recv.at[i], p.dev(a=(p.a + j) % p.A))

    def unit_copy(self, core, stage, j, u, sender):
        p = self.p
        n1, n2 = (p.B, p.Y) if core == 0 else (p.Y, p.B)
        if stage == 1:
            i = j - 1
            first, second = (0 if sender else -j), 0
        else:
            i = (n1 - 1) + (j - 1) * n1 + u
            first, second = u, (0 if sender else -j)
        ry, rb = (second, first) if core == 0 else (first, second)
        digit_b = (core == 0) == (stage == 1)
        dev = p.dev(b=(p.b + j) % p.B) if digit_b else p.dev(y=(p.y + j) % p.Y)
        ref = self.unit(ry % p.Y, rb % p.B, p.c)
        i += p.A - 1
        return remote(ref, ref, self.send.at[i], self.recv.at[i], dev), (ry % p.Y, rb % p.B)

    def twin_copy(self, ry, rb, sender):
        p = self.p
        i = (p.A - 1) + (p.Y * p.B - 1) + ry * p.B + rb
        ref = self.unit(ry, rb, p.c if sender else 1 - p.c)
        return remote(ref, ref, self.send.at[i], self.recv.at[i], p.dev(c=1 - p.c))

    def start(self):
        self.local_copy().start()
        for j in range(1, self.p.A):
            self.a_copy(j, True).start()

    def step1(self):
        p = self.p
        self.local_copy().wait()
        for j in range(1, p.A):
            self.a_copy(j, False).wait_recv()

        def body(core):
            n1 = p.B if core == 0 else p.Y
            for j in range(1, n1):
                self.unit_copy(core, 1, j, 0, True)[0].start()

        p.both(body)
        self.twin_copy(0, 0, True).start()

    def step2(self):
        p = self.p

        def body(core):
            n1, n2 = (p.B, p.Y) if core == 0 else (p.Y, p.B)
            arrived = []
            for j in range(1, n1):
                copy, unit = self.unit_copy(core, 1, j, 0, False)
                copy.wait_recv()
                arrived.append(unit)
            for u in range(n1):
                for j in range(1, n2):
                    self.unit_copy(core, 2, j, u, True)[0].start()
            for unit in arrived:
                self.twin_copy(*unit, True).start()

        p.both(body)

    def step3(self):
        p = self.p

        def body(core):
            n1, n2 = (p.B, p.Y) if core == 0 else (p.Y, p.B)
            for u in range(n1):
                for j in range(1, n2):
                    copy, unit = self.unit_copy(core, 2, j, u, False)
                    copy.wait_recv()
                    self.twin_copy(*unit, True).start()

        p.both(body)

    def finish(self):
        p = self.p
        for ry in range(p.Y):
            for rb in range(p.B):
                self.twin_copy(ry, rb, False).wait_recv()
                self.twin_copy(ry, rb, True).wait_send()
        for j in range(1, p.A):
            self.a_copy(j, True).wait_send()

        def body(core):
            n1, n2 = (p.B, p.Y) if core == 0 else (p.Y, p.B)
            for j in range(1, n1):
                self.unit_copy(core, 1, j, 0, True)[0].wait_send()
            for u in range(n1):
                for j in range(1, n2):
                    self.unit_copy(core, 2, j, u, True)[0].wait_send()

        p.both(body)


class Reduce:
    @staticmethod
    def slots(sizes):
        Y, A, B = sizes
        return max((Y - 1) * B, (B - 1) * Y)

    @staticmethod
    def scratch(sizes, r, c, dtype):
        Y, A, B = sizes
        n = 1 + Y * B - 1 + (A - 1)
        return [
            pltpu.VMEM((Y * A, B, r, c), dtype),
            pltpu.VMEM((Y * A, B, r, c), dtype),
            pltpu.VMEM((Reduce.slots(sizes) * A, r, c), dtype),
            pltpu.VMEM((max(Y - 1, B - 1) * A, r, c), dtype),
            pltpu.VMEM((A - 1, r, c), dtype),
            pltpu.SemaphoreType.DMA((n,)),
            pltpu.SemaphoreType.DMA((n,)),
            pltpu.SemaphoreType.DMA((1,)),
        ]

    def __init__(self, place, partial, out, own, land1, land2, land3, land4, send, recv, local):
        self.p, self.partial, self.out = place, partial, out
        self.own, self.land1, self.land2, self.land3, self.land4 = own, land1, land2, land3, land4
        self.send, self.recv, self.local = send, recv, local

    def twin(self):
        p = self.p
        return remote(
            self.partial.at[:, :, 1 - p.c], self.land1, self.send.at[0], self.recv.at[0], p.dev(c=1 - p.c)
        )

    def local_copy(self):
        return pltpu.make_async_copy(self.partial.at[:, :, self.p.c], self.own, self.local.at[0])

    def order(self, core):
        p = self.p
        return (p.Y, p.B) if core == 0 else (p.B, p.Y)

    def rel(self, core, first, second):
        p = self.p
        ry, rb = (first, second) if core == 0 else (second, first)
        return (p.y + ry) % p.Y, (p.b + rb) % p.B

    def peer(self, core, stage, j):
        p = self.p
        if (core == 0) == (stage == 1):
            return p.dev(y=(p.y + j) % p.Y)
        return p.dev(b=(p.b + j) % p.B)

    def copy1(self, core, j, u):
        p = self.p
        n1, n2 = self.order(core)
        yy, bb = self.rel(core, j, u)
        slot = (j - 1) * n2 + u
        i = 1 + slot
        return remote(
            self.own.at[pl.ds(yy * p.A, p.A), bb],
            self.land2.at[pl.ds(slot * p.A, p.A)],
            self.send.at[i],
            self.recv.at[i],
            self.peer(core, 1, j),
        )

    def copy2(self, core, j):
        p = self.p
        n1, n2 = self.order(core)
        yy, bb = self.rel(core, 0, j)
        i = 1 + (n1 - 1) * n2 + (j - 1)
        return remote(
            self.own.at[pl.ds(yy * p.A, p.A), bb],
            self.land3.at[pl.ds((j - 1) * p.A, p.A)],
            self.send.at[i],
            self.recv.at[i],
            self.peer(core, 2, j),
        )

    def copy3(self, j):
        p = self.p
        i = 1 + p.Y * p.B - 1 + (j - 1)
        a = (p.a + j) % p.A
        return remote(
            self.own.at[p.y * p.A + a, p.b], self.land4.at[j - 1], self.send.at[i], self.recv.at[i], p.dev(a=a)
        )

    def start(self):
        self.twin().start()
        self.local_copy().start()

    def step1(self):
        p = self.p
        self.local_copy().wait()
        self.twin().wait_recv()

        def add(i, _):
            for b in range(p.B):
                total = self.own[i, b].astype(jnp.float32) + self.land1[i, b].astype(jnp.float32)
                self.own[i, b] = total.astype(self.own.dtype)
            return 0

        lax.fori_loop(0, p.Y * p.A, add, 0)

        def body(core):
            n1, n2 = self.order(core)
            for j in range(1, n1):
                for u in range(n2):
                    self.copy1(core, j, u).start()

        p.both(body)

    def step2(self):
        p = self.p

        def body(core):
            n1, n2 = self.order(core)
            for j in range(1, n1):
                for u in range(n2):
                    self.copy1(core, j, u).wait_recv()
            for u in range(n2):
                yy, bb = self.rel(core, 0, u)

                def add(i, _):
                    total = self.own[yy * p.A + i, bb].astype(jnp.float32)
                    for j in range(1, n1):
                        total += self.land2[((j - 1) * n2 + u) * p.A + i].astype(jnp.float32)
                    self.own[yy * p.A + i, bb] = total.astype(self.own.dtype)
                    return 0

                lax.fori_loop(0, p.A, add, 0)
            for j in range(1, n2):
                self.copy2(core, j).start()

        p.both(body)

    def step3(self):
        p = self.p

        def body(core):
            n1, n2 = self.order(core)
            for j in range(1, n2):
                self.copy2(core, j).wait_recv()

            def add(i, _):
                total = self.own[p.y * p.A + i, p.b].astype(jnp.float32)
                for j in range(1, n2):
                    total += self.land3[(j - 1) * p.A + i].astype(jnp.float32)
                self.own[p.y * p.A + i, p.b] = total.astype(self.own.dtype)
                return 0

            lax.fori_loop(0, p.A, add, 0)

        p.both(body)
        for j in range(1, p.A):
            self.copy3(j).start()

    def finish(self):
        p = self.p
        total = self.own[p.y * p.A + p.a, p.b].astype(jnp.float32)
        for j in range(1, p.A):
            self.copy3(j).wait_recv()
            total += self.land4[j - 1].astype(jnp.float32)
        self.out[...] = total
        self.twin().wait_send()
        for j in range(1, p.A):
            self.copy3(j).wait_send()

        def body(core):
            n1, n2 = self.order(core)
            for j in range(1, n1):
                for u in range(n2):
                    self.copy1(core, j, u).wait_send()
            for j in range(1, n2):
                self.copy2(core, j).wait_send()

        p.both(body)


def gather_kernel(sizes, n, *refs):
    shards, fulls, sems = refs[:n], refs[n : 2 * n], refs[2 * n :]
    place = Place(sizes)
    place.barrier()
    gathers = [Gather(place, shards[k], fulls[k], *sems[3 * k : 3 * k + 3]) for k in range(n)]
    for g in gathers:
        g.start()
    for g in gathers:
        g.step1()
    for g in gathers:
        g.step2()
    for g in gathers:
        g.step3()
    for g in gathers:
        g.finish()


def gather_call(sizes, shards, collective_id):
    Y, A, B = sizes
    n = len(shards)
    shapes = [jax.ShapeDtypeStruct((Y * A, B, 2, *s.shape), s.dtype) for s in shards]
    return pl.pallas_call(
        functools.partial(gather_kernel, sizes, n),
        out_shape=shapes,
        in_specs=[ANY] * n,
        out_specs=[ANY] * n,
        scratch_shapes=[s for _ in range(n) for s in Gather.sems(sizes)],
        compiler_params=pltpu.CompilerParams(
            collective_id=collective_id, has_side_effects=True, vmem_limit_bytes=LIMIT
        ),
        name="gather",
    )(*shards)


def reduce_kernel(sizes, n, *refs):
    partials, outs, scratch = refs[:n], refs[n : 2 * n], refs[2 * n :]
    place = Place(sizes)
    place.barrier()
    sums = [Reduce(place, partials[k], outs[k], *scratch[8 * k : 8 * k + 8]) for k in range(n)]
    for s in sums:
        s.start()
    for s in sums:
        s.step1()
    for s in sums:
        s.step2()
    for s in sums:
        s.step3()
    for s in sums:
        s.finish()


def reduce_call(sizes, partials, collective_id):
    Y, A, B = sizes
    n = len(partials)
    partials = [x.reshape(Y * A, B, 2, *x.shape[1:]) for x in partials]
    shapes = [jax.ShapeDtypeStruct(x.shape[3:], jnp.float32) for x in partials]
    return pl.pallas_call(
        functools.partial(reduce_kernel, sizes, n),
        out_shape=shapes,
        in_specs=[ANY] * n,
        out_specs=[VMEM] * n,
        scratch_shapes=[
            s for x in partials for s in Reduce.scratch(sizes, x.shape[3], x.shape[4], x.dtype)
        ],
        compiler_params=pltpu.CompilerParams(
            collective_id=collective_id, has_side_effects=True, vmem_limit_bytes=LIMIT
        ),
        name="reduce",
    )(*partials)


def mesh_sizes(dp, fsdp):
    chips = fsdp // 2
    across = math.gcd(chips, 4)
    return (dp, across, chips // across)


def block_shape(entries, width):
    rows = entries // width
    return (rows, width) if rows % 8 == 0 else (entries // 128, 128)


TILE = 16


def pack_small(vectors, hidden, table):
    lanes = 128
    rows = [jnp.pad(v, (0, lanes - v.shape[0])) for v in vectors]
    rows.append(jnp.pad(hidden, (0, lanes - hidden.shape[0])))
    table_rows = -(-table.shape[0] // lanes)
    rows.append(jnp.pad(table, (0, table_rows * lanes - table.shape[0])))
    flat = jnp.concatenate(rows)
    return jnp.pad(flat, (0, TILE * lanes - flat.shape[0])).reshape(TILE, lanes)


norm_eps = 1e-06


RB = 200
NEG = -1e30
HEAD_QUAD = 4


def params_of(limit=LIMIT, **kw):
    return pltpu.CompilerParams(vmem_limit_bytes=limit, **kw)


def row_norm(values):
    average = jnp.mean(values, axis=-1, keepdims=True)
    centred = values - average
    variance = jnp.mean(centred * centred, axis=-1, keepdims=True)
    inverse = lax.rsqrt(variance + norm_eps)
    return centred * inverse, inverse


def bias_build(tab_ref, bias_ref, rolled, spread, seq_len):
    side = GRID
    span = 2 * side - 1
    wide = 384
    tab = tab_ref[...]
    for x in range(side):
        rolled[pl.ds(x * 16, 16), :] = pltpu.roll(tab, (768 - x) % 768, 1).astype(jnp.bfloat16)
    m = lax.broadcasted_iota(jnp.int32, (768, wide), 0)
    n = lax.broadcasted_iota(jnp.int32, (768, wide), 1)
    pick = (m == span * (span - 1 - n // side) + side - 1 - n % side) & (n < span * side)
    onehot = jnp.where(pick, 1.0, 0.0).astype(jnp.bfloat16)
    picked = jnp.dot(rolled[...], onehot, preferred_element_type=jnp.float32)
    for n in range(wide // 128):
        spread[n] = picked[:, n * 128 : n * 128 + 128]
    lane = lax.broadcasted_iota(jnp.int32, (16, 768), 1)
    base = span * span
    row_first = jnp.sum(jnp.where(lane == base, tab, 0.0), axis=1, keepdims=True)
    col_first = jnp.sum(jnp.where(lane == base + 1, tab, 0.0), axis=1, keepdims=True)
    corner = jnp.sum(jnp.where(lane == base + 2, tab, 0.0), axis=1, keepdims=True)
    cols = lax.broadcasted_iota(jnp.int32, (side, 256), 1)
    top = lax.broadcasted_iota(jnp.int32, (1, 256), 1)
    for h in range(HEADS):
        rows = jnp.concatenate(
            [spread[n, pl.ds(h, side, stride=16), :] for n in range(wide // 128)], axis=1
        )
        first = col_first[h : h + 1, :]
        for y in range(side):
            block = pltpu.roll(rows, (1 - (side - 1 - y) * side) % wide, 1)[:, :256]
            block = jnp.where(cols == 0, first, jnp.where(cols < seq_len, block, NEG))
            bias_ref[h, pl.ds(1 + side * y, side), :] = block[:, :RB]
        line = jnp.where(top == 0, corner[h : h + 1, :], row_first[h : h + 1, :])
        line = jnp.where(top < seq_len, line, NEG)
        bias_ref[h, 0:1, :] = line[:, :RB]
        bias_ref[h, pl.ds(seq_len, RB - seq_len), :] = jnp.where(
            lax.broadcasted_iota(jnp.int32, (RB - seq_len, RB), 1) < seq_len, 0.0, NEG
        )


def attn_forward_kernel(
    patches, mask, vecs, tab, qkv_w, out_w,
    normed_o, qkv_o, probs_o, att_o, branch_o, middle_o,
    x_s, bias_s, rolled, spread,
):
    images, seq_len, dim = patches.shape
    bias_build(tab, bias_s, rolled, spread, seq_len)
    token, gain, shift = vecs[0:1, :], vecs[1:2, :], vecs[2:3, :]

    def load(i, _):
        at = pl.multiple_of(i * RB, 8)
        x_s[pl.ds(at + RB - 8, 8), :] = jnp.zeros((8, dim), jnp.float32)
        rows = patches[i].astype(jnp.float32)
        x_s[pl.ds(at, seq_len), :] = jnp.where(mask[i] > 0.5, token, rows)
        normal, _ = row_norm(x_s[pl.ds(at, RB), :])
        normed_o[pl.ds(at, RB), :] = (normal * gain + shift).astype(jnp.bfloat16)
        return 0

    lax.fori_loop(0, images, load, 0)
    step = 256

    def project(j, _):
        col = pl.multiple_of(j * step, step)
        value = jnp.dot(normed_o[...], qkv_w[:, pl.ds(col, step)], preferred_element_type=jnp.float32)
        part = j // (dim // step)
        inner = pl.multiple_of((j % (dim // step)) * step, step)
        qb = vecs[3:4, pl.ds(inner, step)]
        vb = vecs[4:5, pl.ds(inner, step)]
        add = jnp.where(part == 0, qb, jnp.where(part == 2, vb, 0.0))
        scale = jnp.where(part == 0, 0.125, 1.0)
        qkv_o[:, pl.ds(col, step)] = ((value + add) * scale).astype(jnp.bfloat16)
        return 0

    lax.fori_loop(0, 3 * dim // step, project, 0)
    lane = lax.broadcasted_iota(jnp.int32, (1, step), 1) // 64

    def attend(n, _):
        i, quad = n // 3, n % 3
        at = pl.multiple_of(i * RB, 8)
        col = pl.multiple_of(quad * step, step)
        q = qkv_o[pl.ds(at, RB), pl.ds(col, step)]
        k = qkv_o[pl.ds(at, RB), pl.ds(dim + col, step)]
        v = qkv_o[pl.ds(at, RB), pl.ds(2 * dim + col, step)]
        att = jnp.zeros((RB, step), jnp.float32)
        for j in range(HEAD_QUAD):
            mine = lane == j
            qj = jnp.where(mine, q, jnp.zeros_like(q))
            s = lax.dot_general(qj, k, (((1,), (1,)), ((), ())), preferred_element_type=jnp.float32)
            s = s + bias_s[quad * HEAD_QUAD + j]
            e = jnp.exp(s - jnp.max(s, axis=1, keepdims=True))
            p = (e / jnp.sum(e, axis=1, keepdims=True)).astype(jnp.bfloat16)
            probs_o[i * HEADS + quad * HEAD_QUAD + j] = p
            o = jnp.dot(p, v, preferred_element_type=jnp.float32)
            att = jnp.where(mine, o, att)
        att_o[pl.ds(at, RB), pl.ds(col, step)] = att.astype(jnp.bfloat16)
        return 0

    lax.fori_loop(0, images * 3, attend, 0)

    def leave(j, _):
        col = pl.multiple_of(j * step, step)
        value = jnp.dot(att_o[...], out_w[:, pl.ds(col, step)], preferred_element_type=jnp.float32)
        value = value + vecs[5:6, pl.ds(col, step)]
        branch_o[:, pl.ds(col, step)] = value
        middle_o[:, pl.ds(col, step)] = x_s[:, pl.ds(col, step)] + vecs[6:7, pl.ds(col, step)] * value
        return 0

    lax.fori_loop(0, dim // step, leave, 0)


def attn_forward(patches, mask, vecs, tab, qkv_w, out_w):
    images, seq_len, dim = patches.shape
    rows = images * RB
    f32, bf16 = jnp.float32, jnp.bfloat16
    S = jax.ShapeDtypeStruct
    return pl.pallas_call(
        attn_forward_kernel,
        out_shape=[
            S((rows, dim), bf16), S((rows, 3 * dim), bf16), S((images * HEADS, RB, RB), bf16),
            S((rows, dim), bf16), S((rows, dim), f32), S((rows, dim), f32),
        ],
        in_specs=[VMEM] * 6,
        out_specs=[VMEM] * 6,
        scratch_shapes=[
            pltpu.VMEM((rows, dim), f32), pltpu.VMEM((HEADS, RB, RB), f32),
            pltpu.VMEM((GRID * 16, 768), bf16), pltpu.VMEM((3, GRID * 16, 128), f32),
        ],
        compiler_params=params_of(),
        name="attn_fwd",
    )(patches, mask, vecs, tab, qkv_w, out_w)


def contract(left, right, dim_left, dim_right):
    return lax.dot_general(
        left, right, (((dim_left,), (dim_right,)), ((), ())), preferred_element_type=jnp.float32
    )


def mlp_kernel(
    middle, cotangent, mask, vecs, up_b, up_w, down_w,
    layer_o, grad_middle_o, up_grad_o, down_grad_o, vec_o, up_b_o,
    go_s, gd_s, xn_s, down_s, dx_s,
):
    images, seq_len, dim = cotangent.shape
    rows = images * RB
    hidden_dim = up_w.shape[1]
    post_g, post_s = vecs[7:8, :], vecs[8:9, :]
    down_b, mlp_g = vecs[9:10, :], vecs[10:11, :]
    step = 256
    vec_o[...] = jnp.zeros_like(vec_o)
    down_s[...] = jnp.zeros_like(down_s)
    dx_s[...] = jnp.zeros_like(dx_s)

    def load(i, _):
        at = pl.multiple_of(i * RB, 8)
        go_s[pl.ds(at + RB - 8, 8), :] = jnp.zeros((8, dim), jnp.float32)
        grad = cotangent[i].astype(jnp.float32)
        go_s[pl.ds(at, seq_len), :] = jnp.where(mask[i] > 0.5, grad, 0.0)
        grad = go_s[pl.ds(at, RB), :] * mlp_g
        vec_o[9:10, :] += jnp.sum(grad, axis=0, keepdims=True)
        gd_s[pl.ds(at, RB), :] = grad.astype(jnp.bfloat16)
        normal, _ = row_norm(middle[pl.ds(at, RB), :])
        xn_s[pl.ds(at, RB), :] = (normal * post_g + post_s).astype(jnp.bfloat16)
        return 0

    lax.fori_loop(0, images, load, 0)

    def chunk(j, _):
        col = pl.multiple_of(j * step, step)
        up_c = up_w[:, pl.ds(col, step)]
        down_c = down_w[pl.ds(col, step), :]
        xn, gd = xn_s[...], gd_s[...]
        up = jnp.dot(xn, up_c, preferred_element_type=jnp.float32) + up_b[0:1, pl.ds(col, step)]
        cdf = 0.5 * (1.0 + lax.erf(up * 0.7071067811865476))
        hidden = (up * cdf).astype(jnp.bfloat16)
        slope = cdf + up * jnp.exp(-0.5 * up * up) * 0.3989422804014327
        grad = contract(gd, down_c, 1, 1) * slope
        up_b_o[0:1, pl.ds(col, step)] = jnp.sum(grad, axis=0, keepdims=True)
        gu = grad.astype(jnp.bfloat16)
        down_s[...] += jnp.dot(hidden, down_c, preferred_element_type=jnp.float32)
        dx_s[...] += contract(gu, up_c, 1, 1)
        down_grad_o[pl.ds(col, step), :] = contract(hidden, gd, 0, 0).astype(jnp.bfloat16)
        up_grad_o[:, pl.ds(col, step)] = contract(xn, gu, 0, 0).astype(jnp.bfloat16)
        return 0

    lax.fori_loop(0, hidden_dim // step, chunk, 0)

    def leave(i, _):
        at = pl.multiple_of(i * RB, 8)
        go = go_s[pl.ds(at, RB), :]
        mid = middle[pl.ds(at, RB), :]
        down_rows = down_s[pl.ds(at, RB), :] + down_b
        layer_o[i] = (mid + mlp_g * down_rows)[:seq_len].astype(jnp.bfloat16)
        vec_o[10:11, :] += jnp.sum(go * down_rows, axis=0, keepdims=True)
        grad = dx_s[pl.ds(at, RB), :]
        normal, inverse = row_norm(mid)
        vec_o[7:8, :] += jnp.sum(grad * normal, axis=0, keepdims=True)
        vec_o[8:9, :] += jnp.sum(grad, axis=0, keepdims=True)
        grad_middle_o[pl.ds(at, RB), :] = go + norm_back(grad, normal, inverse, post_g)
        return 0

    lax.fori_loop(0, images, leave, 0)


def mlp(middle, cotangent, mask, vecs, up_b, up_w, down_w):
    images, seq_len, dim = cotangent.shape
    rows = images * RB
    f32, bf16 = jnp.float32, jnp.bfloat16
    S = jax.ShapeDtypeStruct
    return pl.pallas_call(
        mlp_kernel,
        out_shape=[
            S(cotangent.shape, bf16), S((rows, dim), f32), S(up_w.shape, bf16), S(down_w.shape, bf16),
            S((16, dim), f32), S(up_b.shape, f32),
        ],
        in_specs=[VMEM] * 7,
        out_specs=[VMEM] * 6,
        scratch_shapes=[
            pltpu.VMEM((rows, dim), f32), pltpu.VMEM((rows, dim), bf16), pltpu.VMEM((rows, dim), bf16),
            pltpu.VMEM((rows, dim), f32), pltpu.VMEM((rows, dim), f32),
        ],
        compiler_params=params_of(),
        name="mlp",
    )(middle, cotangent, mask, vecs, up_b, up_w, down_w)


def table_build(db, out_ref, rows_s, seq_len):
    side = GRID
    span = 2 * side - 1
    wide = 384
    rows_s[...] = jnp.zeros_like(rows_s)
    lane = lax.broadcasted_iota(jnp.int32, (1, RB), 1)
    out_lane = lax.broadcasted_iota(jnp.int32, (1, 768), 1)
    base = span * span
    for h in range(HEADS):
        total = jnp.zeros((side, wide), jnp.float32)
        for y in range(side):
            block = db[h, pl.ds(1 + side * y, side), :]
            block = jnp.where((lane > 0) & (lane < seq_len), block, 0.0)
            block = jnp.concatenate([block, jnp.zeros((side, wide - RB), jnp.float32)], axis=1)
            total += pltpu.roll(block, ((side - 1 - y) * side - 1) % wide, 1)
        for n in range(wide // 128):
            rows_s[n, pl.ds(h, side, stride=16), :] = total[:, n * 128 : n * 128 + 128]
    m = lax.broadcasted_iota(jnp.int32, (wide, 768), 1)
    n = lax.broadcasted_iota(jnp.int32, (wide, 768), 0)
    pick = (m == span * (span - 1 - n // side) + side - 1 - n % side) & (n < span * side)
    onehot = jnp.where(pick, 1.0, 0.0).astype(jnp.bfloat16)
    total = jnp.zeros((16, 768), jnp.float32)
    for x in range(side):
        rows = jnp.concatenate([rows_s[k, pl.ds(x * 16, 16), :] for k in range(wide // 128)], axis=1)
        upper = rows.astype(jnp.bfloat16)
        lower = (rows - upper.astype(jnp.float32)).astype(jnp.bfloat16)
        part = jnp.dot(upper, onehot, preferred_element_type=jnp.float32)
        part += jnp.dot(lower, onehot, preferred_element_type=jnp.float32)
        total += pltpu.roll(part, x, 1)
    out_ref[...] = total
    for h in range(HEADS):
        top = db[h, 0:1, :]
        corner = jnp.sum(jnp.where(lane == 0, top, 0.0), axis=1, keepdims=True)
        first_row = jnp.sum(jnp.where(lane > 0, top, 0.0), axis=1, keepdims=True)
        col = jnp.sum(db[h], axis=0, keepdims=True)
        first_col = jnp.sum(jnp.where(lane == 0, col, 0.0), axis=1, keepdims=True) - corner
        line = out_ref[h : h + 1, :]
        line = jnp.where(out_lane == base, first_row, line)
        line = jnp.where(out_lane == base + 1, first_col, line)
        out_ref[h : h + 1, :] = jnp.where(out_lane == base + 2, corner, line)


def attn_backward_kernel(
    grad_middle, branch, att, qkv, probs, normed, patches, mask, vecs, qkv_w, out_w,
    patch_o, qkv_grad_o, out_grad_o, vec_o, tab_o,
    gb_s, ga_s, gproj_s, gnp_s, db_s, rows_s,
):
    images, seq_len, dim = patches.shape
    token, gain, scale = vecs[0:1, :], vecs[1:2, :], vecs[6:7, :]
    step = 256
    vec_o[...] = jnp.zeros_like(vec_o)
    db_s[...] = jnp.zeros_like(db_s)

    def enter(i, _):
        at = pl.multiple_of(i * RB, 8)
        grad = grad_middle[pl.ds(at, RB), :]
        vec_o[6:7, :] += jnp.sum(grad * branch[pl.ds(at, RB), :], axis=0, keepdims=True)
        grad = grad * scale
        vec_o[5:6, :] += jnp.sum(grad, axis=0, keepdims=True)
        gb_s[pl.ds(at, RB), :] = grad.astype(jnp.bfloat16)
        return 0

    lax.fori_loop(0, images, enter, 0)

    def out_part(j, _):
        col = pl.multiple_of(j * step, step)
        ga_s[:, pl.ds(col, step)] = contract(gb_s[...], out_w[pl.ds(col, step), :], 1, 1).astype(jnp.bfloat16)
        out_grad_o[:, pl.ds(col, step)] = contract(att[...], gb_s[:, pl.ds(col, step)], 0, 0).astype(jnp.bfloat16)
        return 0

    lax.fori_loop(0, dim // step, out_part, 0)
    lane = lax.broadcasted_iota(jnp.int32, (1, step), 1) // 64

    def attend(n, _):
        quad, i = n // images, n % images
        at = pl.multiple_of(i * RB, 8)
        col = pl.multiple_of(quad * step, step)
        q = qkv[pl.ds(at, RB), pl.ds(col, step)]
        k = qkv[pl.ds(at, RB), pl.ds(dim + col, step)]
        v = qkv[pl.ds(at, RB), pl.ds(2 * dim + col, step)]
        ga = ga_s[pl.ds(at, RB), pl.ds(col, step)]
        zero = jnp.zeros((RB, step), jnp.float32)
        gq, gk, gv = zero, zero, zero
        for j in range(HEAD_QUAD):
            mine = lane == j
            h = quad * HEAD_QUAD + j
            p = probs[i * HEADS + h]
            gp = contract(jnp.where(mine, ga, jnp.zeros_like(ga)), v, 1, 1)
            gv = jnp.where(mine, contract(p, ga, 0, 0), gv)
            pf = p.astype(jnp.float32)
            gs = pf * (gp - jnp.sum(pf * gp, axis=1, keepdims=True))
            db_s[h] += gs
            low = gs.astype(jnp.bfloat16)
            gq = jnp.where(mine, jnp.dot(low, k, preferred_element_type=jnp.float32), gq)
            gk = jnp.where(mine, contract(low, q, 0, 0), gk)
        gq = gq * 0.125
        vec_o[3:4, pl.ds(col, step)] += jnp.sum(gq, axis=0, keepdims=True)
        vec_o[4:5, pl.ds(col, step)] += jnp.sum(gv, axis=0, keepdims=True)
        gproj_s[pl.ds(at, RB), pl.ds(col, step)] = gq.astype(jnp.bfloat16)
        gproj_s[pl.ds(at, RB), pl.ds(dim + col, step)] = gk.astype(jnp.bfloat16)
        gproj_s[pl.ds(at, RB), pl.ds(2 * dim + col, step)] = gv.astype(jnp.bfloat16)
        return 0

    lax.fori_loop(0, images * 3, attend, 0)

    def qkv_part(j, _):
        col = pl.multiple_of(j * step, step)
        qkv_grad_o[:, pl.ds(col, step)] = contract(normed[...], gproj_s[:, pl.ds(col, step)], 0, 0).astype(
            jnp.bfloat16
        )
        return 0

    lax.fori_loop(0, 3 * dim // step, qkv_part, 0)

    def back(j, _):
        col = pl.multiple_of(j * step, step)
        gnp_s[:, pl.ds(col, step)] = contract(gproj_s[...], qkv_w[pl.ds(col, step), :], 1, 1)
        return 0

    lax.fori_loop(0, dim // step, back, 0)

    def leave(i, _):
        at = pl.multiple_of(i * RB, 8)
        here = mask[i] > 0.5
        rows = jnp.where(here, token, patches[i].astype(jnp.float32))
        normal, inverse = row_norm(rows)
        grad = gnp_s[pl.ds(at, RB), :][:seq_len]
        vec_o[1:2, :] += jnp.sum(grad * normal, axis=0, keepdims=True)
        vec_o[2:3, :] += jnp.sum(grad, axis=0, keepdims=True)
        grad = grad_middle[pl.ds(at, RB), :][:seq_len] + norm_back(grad, normal, inverse, gain)
        vec_o[0:1, :] += jnp.sum(jnp.where(here, grad, 0.0), axis=0, keepdims=True)
        patch_o[i] = jnp.where(here, 0.0, grad).astype(jnp.bfloat16)
        return 0

    lax.fori_loop(0, images, leave, 0)
    table_build(db_s, tab_o, rows_s, seq_len)


def attn_backward(grad_middle, branch, att, qkv, probs, normed, patches, mask, vecs, qkv_w, out_w):
    images, seq_len, dim = patches.shape
    rows = images * RB
    f32, bf16 = jnp.float32, jnp.bfloat16
    S = jax.ShapeDtypeStruct
    return pl.pallas_call(
        attn_backward_kernel,
        out_shape=[
            S(patches.shape, bf16), S(qkv_w.shape, bf16), S(out_w.shape, bf16), S((16, dim), f32),
            S((16, 768), f32),
        ],
        in_specs=[VMEM] * 11,
        out_specs=[VMEM] * 5,
        scratch_shapes=[
            pltpu.VMEM((rows, dim), bf16), pltpu.VMEM((rows, dim), bf16), pltpu.VMEM((rows, 3 * dim), bf16),
            pltpu.VMEM((rows, dim), f32), pltpu.VMEM((HEADS, RB, RB), f32),
            pltpu.VMEM((3, GRID * 16, 128), f32),
        ],
        compiler_params=params_of(),
        name="attn_bwd",
    )(grad_middle, branch, att, qkv, probs, normed, patches, mask, vecs, qkv_w, out_w)


def norm_back(grad_normed, normal, inverse, gain):
    scaled = grad_normed * gain
    first_mean = jnp.mean(scaled, axis=-1, keepdims=True)
    second_mean = jnp.mean(scaled * normal, axis=-1, keepdims=True)
    return inverse * (scaled - first_mean - normal * second_mean)


def per_device(
    patches, patch_mask, cotangent, mask_token, pre_gain, pre_shift, qkv_weight, query_bias, value_bias,
    rel_table, out_weight, out_bias, attn_scale, post_gain, post_shift, up_weight, up_bias, down_weight,
    down_bias, mlp_scale,
):
    images, seq_len, dim = patches.shape
    table_rows = (2 * GRID - 1) ** 2 + 3
    devices = lax.axis_size(("dp", "fsdp"))
    sizes = mesh_sizes(lax.axis_size("dp"), lax.axis_size("fsdp"))
    vec_shards = (
        mask_token, pre_gain, pre_shift, query_bias, value_bias, out_bias, attn_scale,
        post_gain, post_shift, down_bias, mlp_scale,
    )
    small = pack_small(vec_shards, up_bias, rel_table)
    widths = (3 * dim, dim, FF, dim)
    mats = (qkv_weight, out_weight, up_weight, down_weight)
    blocks = [m.reshape(block_shape(m.shape[0], w)) for m, w in zip(mats, widths)]
    small_full, *mats_full = gather_call(sizes, [small] + blocks, 0)
    qkv_w, out_w, up_w, down_w = [m.reshape(-1, w) for m, w in zip(mats_full, widths)]
    rows_full = small_full.reshape(devices, TILE, 128).astype(jnp.float32)
    per_vec = mask_token.shape[0]
    vecs = jnp.transpose(rows_full[:, :11, :per_vec], (1, 0, 2)).reshape(11, dim)
    vecs = jnp.pad(vecs, ((0, 5), (0, 0)))
    up_b = rows_full[:, 11, : up_bias.shape[0]].reshape(1, FF)
    table = rows_full[:, 12:].reshape(devices, -1)[:, : rel_table.shape[0]].reshape(-1)
    table = table[: table_rows * HEADS].reshape(table_rows, HEADS).T
    table = jnp.pad(table, ((0, 16 - HEADS), (0, 768 - table_rows)))
    mask = patch_mask.astype(jnp.float32)[:, :, None]
    normed, qkv, probs, att, branch, middle = attn_forward(patches, mask, vecs, table, qkv_w, out_w)
    layer_out, grad_middle, up_grad, down_grad, vec_mlp, up_b_grad = mlp(
        middle, cotangent, mask, vecs, up_b, up_w, down_w
    )
    patch_grad, qkv_grad, out_grad, vec_attn, table_grad = attn_backward(
        grad_middle, branch, att, qkv, probs, normed, patches, mask, vecs, qkv_w, out_w
    )
    vec_grad = jnp.concatenate([vec_attn[:7], vec_mlp[7:11]]).reshape(11, devices, per_vec)
    vec_grad = jnp.pad(jnp.transpose(vec_grad, (1, 0, 2)), ((0, 0), (0, 0), (0, 128 - per_vec)))
    up_b_grad = up_b_grad.reshape(devices, 1, -1)
    up_b_grad = jnp.pad(up_b_grad, ((0, 0), (0, 0), (0, 128 - up_b_grad.shape[2])))
    table_flat = table_grad[:HEADS, :table_rows].T.reshape(-1)
    table_flat = jnp.pad(table_flat, (0, devices * rel_table.shape[0] - table_flat.shape[0]))
    table_flat = table_flat.reshape(devices, -1)
    table_flat = jnp.pad(table_flat, ((0, 0), (0, (TILE - 12) * 128 - table_flat.shape[1])))
    small_grad = jnp.concatenate(
        [vec_grad, up_b_grad, table_flat.reshape(devices, TILE - 12, 128)], axis=1
    )
    partials = [
        g.reshape(devices, *b.shape) for g, b in zip((qkv_grad, out_grad, up_grad, down_grad), blocks)
    ]
    *mat_own, small_own = reduce_call(sizes, partials + [small_grad], 1)
    qkv_o, out_o, up_o, down_o = [m.reshape(-1) for m in mat_own]
    vec_o = [small_own[i, :per_vec] for i in range(11)]
    up_bias_o = small_own[11, : up_bias.shape[0]]
    table_o = small_own[12:].reshape(-1)[: rel_table.shape[0]]
    (
        token_o, pre_gain_o, pre_shift_o, query_bias_o, value_bias_o, out_bias_o, attn_scale_o,
        post_gain_o, post_shift_o, down_bias_o, mlp_scale_o,
    ) = vec_o
    return (
        layer_out, patch_grad, token_o, pre_gain_o, pre_shift_o, qkv_o, query_bias_o, value_bias_o,
        table_o, out_o, out_bias_o, attn_scale_o, post_gain_o, post_shift_o, up_o, up_bias_o,
        down_o, down_bias_o, mlp_scale_o,
    )


def solution(mesh):
    split = ("dp", "fsdp")
    rows = P(split, None, None)
    in_specs = (rows, P(split, None), rows) + (P(split),) * 17
    out_specs = (rows, rows) + (P(split),) * 17
    return jax.shard_map(
        per_device, mesh=mesh, in_specs=in_specs, out_specs=out_specs, check_vma=False
    )
```
